512 devices in a mesh: context: 32 (over y, x), tensor: 4 (over z_hi), dp: 4 (over z_lo, core).
Axes of the slice: x: 4, y: 8, z: 8 (z_hi: 4, z_lo: 2; z = z_hi * 2 + z_lo), core: 2. Of those that a mesh axis runs over, the one named last changes fastest.
Arguments:
- grad_out: bfloat16 [4, 8192, 1024], P('dp', 'context', 'tensor'), may hold values from -6 to 6
- inputs: bfloat16 [4, 8192, 1024], P('dp', 'context', 'tensor'), may hold values from -0.03125 to 0.03125
- filt: bfloat16 [8192, 1024], P('context', 'tensor'), may hold values from -0.0625 to 0.0625
Outputs:
- input_grad: bfloat16 [4, 8192, 1024], P('dp', 'context', 'tensor')
- filter_grad: float32 [8192, 1024], P('context', 'tensor')
The draws below stay inside these ranges and needn't reach their ends.
All inputs are finite; a program needn't handle non-finite values.
Results may differ from the reference program's by a relative error of at most 0.001.
Values may be sent and summed in bfloat16 or wider, within the bound.
No kernel may reach another device: no remote copies, remote signals or barrier semaphores. Data moves between devices by JAX's collectives and lax.ppermute only.
A program may use at most 64 MiB of HBM per device.

```python
import jax
import jax.numpy as jnp

CHANNELS = 1024
SEQ = 8192
BATCH = 4


def level_of(stream_key, dims, cuts, low, high):
    def one(dim, blocks):
        steps = jax.random.uniform(jax.random.fold_in(jax.random.fold_in(stream_key, 6), dim), (blocks,), jnp.float32, low / len(cuts), high / len(cuts))
        return jnp.repeat(jnp.exp(steps), dims[dim] // blocks).reshape((-1,) + (1,) * (len(dims) - dim - 1))

    factor_of = one(*cuts[0])
    for cut in cuts[1:]:
        factor_of = factor_of * one(*cut)
    return factor_of


def gaussian(stream_key, dims, deviation, most, pieces=(), dtype=jnp.bfloat16):
    loudness = level_of(stream_key, dims, pieces, -0.22, 0.18) if pieces else 1.0
    values = jax.random.normal(stream_key, dims, jnp.float32) * deviation * loudness
    return jnp.minimum(jnp.maximum(values, -most), most).astype(dtype)


def setup_inputs(seed: int = 0) -> dict:
    key_list = jax.random.split(jax.random.key(seed), 4)
    grad_out = gaussian(key_list[0], (BATCH, SEQ, CHANNELS), 1.0, 6.0, ((0, 4), (1, 32), (2, 4)))
    inputs = gaussian(key_list[1], (BATCH, SEQ, CHANNELS), (BATCH * SEQ) ** -0.5, 0.03125, ((0, 4), (1, 32), (2, 4)))
    filt = gaussian(key_list[2], (SEQ, CHANNELS), SEQ ** -0.5, 0.0625, ((0, 32), (1, 4)))
    return {"grad_out": grad_out, "inputs": inputs, "filt": filt}


def reference(grad_out, inputs, filt):
    padded_length = 2 * grad_out.shape[1]
    spec_grad = jnp.fft.rfft(grad_out.astype(jnp.float32), n=padded_length, axis=1)
    spec_input = jnp.fft.rfft(inputs.astype(jnp.float32), n=padded_length, axis=1)
    spec_filter = jnp.fft.rfft(filt.astype(jnp.float32), n=padded_length, axis=0)
    input_grad = jnp.fft.irfft(spec_grad * jnp.conj(spec_filter)[None], n=padded_length, axis=1)[:, :SEQ]
    summed = jnp.sum(spec_grad * jnp.conj(spec_input), axis=0)
    filter_grad = jnp.fft.irfft(summed, n=padded_length, axis=0)[:SEQ]
    return input_grad.astype(jnp.bfloat16), filter_grad.astype(jnp.float32)
```

```python
import functools
import jax
import jax.numpy as jnp
from jax import lax
from jax.experimental import pallas as pl
from jax.experimental.pallas import tpu as pltpu
from jax.sharding import PartitionSpec as P

F32 = jnp.float32
BF16 = jnp.bfloat16


def nt_dot(left, right):
    return lax.dot_general(left, right, (((1,), (1,)), ((), ())), preferred_element_type=F32)


def spread_row(ref, row, lane):
    return ref[pl.ds(2 * lane + row, 8, stride=0), :]


def build_lags(rows, out_ref):
    sub = lax.broadcasted_iota(jnp.int32, (8, 128), 0)
    lane = lax.broadcasted_iota(jnp.int32, (8, 128), 1)
    masks = [lane < sub + 8 * s for s in range(4)]
    before = [jnp.zeros((8, 128), F32) for _ in range(4)]
    for d in range(32):
        low, high = rows(d)
        pieces = []
        for s in range(4):
            low_turned = pltpu.roll(low, 8 * s, 1, stride=1, stride_axis=0)
            high_turned = pltpu.roll(high, 8 * s, 1, stride=1, stride_axis=0)
            pieces.append(
                jnp.concatenate(
                    [
                        jnp.where(masks[s], before[s], low_turned),
                        jnp.where(masks[s], low_turned, high_turned),
                    ],
                    axis=1,
                )
            )
            before[s] = high_turned
        out_ref[32 * d : 32 * d + 32, :] = jnp.concatenate(pieces, axis=0).astype(BF16)


def build_windows(rows, out_ref):
    sub = lax.broadcasted_iota(jnp.int32, (8, 128), 0)
    lane = lax.broadcasted_iota(jnp.int32, (8, 128), 1)
    shift = 7 - sub
    inside = lane < 128 - 32 * lax.rem(shift, 4)
    early = shift < 4

    def turned(a):
        once = [pltpu.roll(half, 16, 1, stride=16, stride_axis=0) for half in rows(a)]
        return [pltpu.roll(half, 16, 1, stride=16, stride_axis=0) for half in once]

    here = turned(0)
    pair = []
    for a in range(32):
        after = turned(a + 1) if a < 31 else [jnp.zeros((8, 128), F32)] * 2
        first = jnp.where(inside, here[0], here[1])
        second = jnp.where(inside, here[1], after[0])
        third = jnp.where(inside, after[0], after[1])
        pair.append(
            jnp.concatenate(
                [jnp.where(early, first, second), jnp.where(early, second, third)], axis=1
            )
        )
        if a % 2 == 1:
            out_ref[8 * a - 8 : 8 * a + 8, :] = jnp.concatenate(pair, axis=0).astype(BF16)
            pair = []
        here = after


def add_products(window_ref, lag_ref, total_ref):
    for q in range(4):
        part = nt_dot(window_ref[64 * q :, :], lag_ref[256 * q : 256 * q + 256, :])
        size = 256 - 64 * q
        total_ref[0:size, :] += part[:, 0:128]
        total_ref[0 : size - 32, :] += part[32:, 128:256]


def finish(total_ref, flat_ref):
    lane = lax.broadcasted_iota(jnp.int32, (256, 128), 1)
    sub = lax.broadcasted_iota(jnp.int32, (256, 128), 0)
    group = lane // 32
    mixed = total_ref[0:256, :]
    for p in range(1, 4):
        mixed = jnp.where(group == p, total_ref[8 * p : 8 * p + 256, :], mixed)
    mixed = mixed + pltpu.roll(mixed, 64, 1)
    mixed = mixed + pltpu.roll(mixed, 32, 1)
    flat_ref[...] = jnp.where(group == 3 - lax.rem(sub, 4), mixed, 0.0)

    def gathered(first):
        return sum(flat_ref[pl.ds(7 - r, 32, stride=8), :] for r in range(first, first + 4))

    return gathered(0), gathered(4)


def conv_kernel(r_ref, dx_ref, dh_ref, lag_f, lag_x, window, total_dx, total_dh, flat):
    def channel(c, carry):
        def filter_rows(d):
            return (spread_row(r_ref, d * 8 + c, 512), spread_row(r_ref, d * 8 + 4 + c, 512))

        build_lags(filter_rows, lag_f)
        total_dh[...] = jnp.zeros_like(total_dh)

        def batch(b, inner):
            def rows_at(offset):
                def rows(d):
                    row = d * 8 + b * 2 + c
                    return (spread_row(r_ref, row, offset), spread_row(r_ref, row, offset + 128))

                return rows

            build_windows(rows_at(0), window)
            build_lags(rows_at(256), lag_x)
            total_dx[...] = jnp.zeros_like(total_dx)
            add_products(window, lag_f, total_dx)
            add_products(window, lag_x, total_dh)
            low, high = finish(total_dx, flat)
            dx_ref[pl.ds(b * 2 + c, 32, stride=8), :] = low
            dx_ref[pl.ds(256 + b * 2 + c, 32, stride=8), :] = high
            return inner

        lax.fori_loop(0, 4, batch, 0)
        low, high = finish(total_dh, flat)
        dh_ref[pl.ds(c, 32, stride=2), :] = low
        dh_ref[pl.ds(64 + c, 32, stride=2), :] = high
        return carry

    lax.fori_loop(0, 2, channel, 0)


def conv_call(r):
    vmem = pl.BlockSpec(memory_space=pltpu.VMEM)
    return pl.pallas_call(
        conv_kernel,
        out_shape=(
            jax.ShapeDtypeStruct((512, 128), F32),
            jax.ShapeDtypeStruct((128, 128), F32),
        ),
        in_specs=[vmem],
        out_specs=(vmem, vmem),
        scratch_shapes=[
            pltpu.VMEM((1024, 256), BF16),
            pltpu.VMEM((1024, 256), BF16),
            pltpu.VMEM((256, 256), BF16),
            pltpu.VMEM((280, 128), F32),
            pltpu.VMEM((280, 128), F32),
            pltpu.VMEM((256, 128), F32),
        ],
    )(r)


def body(grad_out, inputs, filt):
    turn = lax.axis_index("dp")
    wide = grad_out.shape[2]
    filter_turned = filt.T
    piece = lax.dynamic_slice(filter_turned, (0, 128 * (turn // 2)), (wide, 128))
    packed = jnp.concatenate([grad_out[0].T, inputs[0].T, piece], axis=1).reshape(128, 2, 640)
    arrived = lax.all_to_all(packed, ("context", "dp"), 0, 0, tiled=True)
    lanes = arrived.astype(F32).reshape(256, 5, 128).transpose(1, 0, 2).reshape(1280, 128)
    dx, dh = conv_call(lanes)
    dx = dx.reshape(2, 128, 2, 128).transpose(1, 2, 0, 3).reshape(128, 2, 256)
    dh = dh.reshape(2, 32, 2, 128).transpose(1, 2, 0, 3).reshape(32, 1, 2, 256)
    dh = jnp.broadcast_to(dh, (32, 4, 2, 256)).reshape(128, 2, 256)
    upper = lax.reduce_precision(dh, 8, 7)
    lower = (dh - upper).astype(BF16)
    outgoing = jnp.concatenate([dx.astype(BF16), upper.astype(BF16), lower], axis=2)
    returned = lax.all_to_all(outgoing, ("context", "dp"), 0, 0, tiled=True).reshape(256, 768)
    input_grad = returned[:, 0:256].T
    filter_grad = returned[:, 256:512].astype(F32) + returned[:, 512:768].astype(F32)
    return input_grad[None], filter_grad.T


def solution(mesh):
    return jax.shard_map(
        body,
        mesh=mesh,
        in_specs=(
            P("dp", "context", "tensor"),
            P("dp", "context", "tensor"),
            P("context", "tensor"),
        ),
        out_specs=(P("dp", "context", "tensor"), P("context", "tensor")),
        check_vma=False,
    )
```

```python
import functools
import jax
import jax.numpy as jnp
from jax import lax
from jax.experimental import pallas as pl
from jax.experimental.pallas import tpu as pltpu
from jax.sharding import PartitionSpec as P

F32 = jnp.float32
BF16 = jnp.bfloat16


def nt_dot(left, right):
    return lax.dot_general(left, right, (((1,), (1,)), ((), ())), preferred_element_type=F32)


def spread_row(ref, row, lane):
    return ref[pl.ds(2 * lane + row, 8, stride=0), :]


def build_lags(rows, out_ref):
    sub = lax.broadcasted_iota(jnp.int32, (8, 128), 0)
    lane = lax.broadcasted_iota(jnp.int32, (8, 128), 1)
    masks = [lane < sub + 8 * s for s in range(4)]
    before = [jnp.zeros((8, 128), F32) for _ in range(4)]
    for d in range(32):
        low, high = rows(d)
        pieces = []
        for s in range(4):
            low_turned = pltpu.roll(low, 8 * s, 1, stride=1, stride_axis=0)
            high_turned = pltpu.roll(high, 8 * s, 1, stride=1, stride_axis=0)
            pieces.append(
                jnp.concatenate(
                    [
                        jnp.where(masks[s], before[s], low_turned),
                        jnp.where(masks[s], low_turned, high_turned),
                    ],
                    axis=1,
                )
            )
            before[s] = high_turned
        out_ref[32 * d : 32 * d + 32, :] = jnp.concatenate(pieces, axis=0).astype(BF16)


def build_windows(rows, out_ref):
    sub = lax.broadcasted_iota(jnp.int32, (8, 128), 0)
    lane = lax.broadcasted_iota(jnp.int32, (8, 128), 1)
    shift = 7 - sub
    inside = lane < 128 - 32 * lax.rem(shift, 4)
    early = shift < 4

    def turned(a):
        once = [pltpu.roll(half, 16, 1, stride=16, stride_axis=0) for half in rows(a)]
        return [pltpu.roll(half, 16, 1, stride=16, stride_axis=0) for half in once]

    here = turned(0)
    pair = []
    for a in range(32):
        after = turned(a + 1) if a < 31 else [jnp.zeros((8, 128), F32)] * 2
        first = jnp.where(inside, here[0], here[1])
        second = jnp.where(inside, here[1], after[0])
        third = jnp.where(inside, after[0], after[1])
        pair.append(
            jnp.concatenate(
                [jnp.where(early, first, second), jnp.where(early, second, third)], axis=1
            )
        )
        if a % 2 == 1:
            out_ref[8 * a - 8 : 8 * a + 8, :] = jnp.concatenate(pair, axis=0).astype(BF16)
            pair = []
        here = after


def add_products(window_ref, lag_ref, total_ref):
    for q in range(4):
        part = nt_dot(window_ref[64 * q :, :], lag_ref[256 * q : 256 * q + 256, :])
        size = 256 - 64 * q
        total_ref[0:size, :] += part[:, 0:128]
        total_ref[0 : size - 32, :] += part[32:, 128:256]


def finish(total_ref, flat_ref):
    lane = lax.broadcasted_iota(jnp.int32, (256, 128), 1)
    sub = lax.broadcasted_iota(jnp.int32, (256, 128), 0)
    group = lane // 32
    mixed = total_ref[0:256, :]
    for p in range(1, 4):
        mixed = jnp.where(group == p, total_ref[8 * p : 8 * p + 256, :], mixed)
    mixed = mixed + pltpu.roll(mixed, 64, 1)
    mixed = mixed + pltpu.roll(mixed, 32, 1)
    flat_ref[...] = jnp.where(group == 3 - lax.rem(sub, 4), mixed, 0.0)

    def gathered(first):
        return sum(flat_ref[pl.ds(7 - r, 32, stride=8), :] for r in range(first, first + 4))

    return gathered(0), gathered(4)


def conv_kernel(r_ref, dx_ref, dh_ref, lag_f, lag_x, window, total_dx, total_dh, flat):
    def channel(c, carry):
        def filter_rows(d):
            return (spread_row(r_ref, d * 8 + c, 512), spread_row(r_ref, d * 8 + 4 + c, 512))

        build_lags(filter_rows, lag_f)
        total_dh[...] = jnp.zeros_like(total_dh)

        def batch(b, inner):
            def rows_at(offset):
                def rows(d):
                    row = d * 8 + b * 2 + c
                    return (spread_row(r_ref, row, offset), spread_row(r_ref, row, offset + 128))

                return rows

            build_windows(rows_at(0), window)
            build_lags(rows_at(256), lag_x)
            total_dx[...] = jnp.zeros_like(total_dx)
            add_products(window, lag_f, total_dx)
            add_products(window, lag_x, total_dh)
            low, high = finish(total_dx, flat)
            dx_ref[pl.ds(b * 2 + c, 32, stride=8), :] = low
            dx_ref[pl.ds(256 + b * 2 + c, 32, stride=8), :] = high
            return inner

        lax.fori_loop(0, 4, batch, 0)
        low, high = finish(total_dh, flat)
        dh_ref[pl.ds(c, 32, stride=2), :] = low
        dh_ref[pl.ds(64 + c, 32, stride=2), :] = high
        return carry

    lax.fori_loop(0, 2, channel, 0)


def conv_call(r):
    vmem = pl.BlockSpec(memory_space=pltpu.VMEM)
    return pl.pallas_call(
        conv_kernel,
        out_shape=(
            jax.ShapeDtypeStruct((512, 128), F32),
            jax.ShapeDtypeStruct((128, 128), F32),
        ),
        in_specs=[vmem],
        out_specs=(vmem, vmem),
        scratch_shapes=[
            pltpu.VMEM((1024, 256), BF16),
            pltpu.VMEM((1024, 256), BF16),
            pltpu.VMEM((256, 256), BF16),
            pltpu.VMEM((280, 128), F32),
            pltpu.VMEM((280, 128), F32),
            pltpu.VMEM((256, 128), F32),
        ],
        compiler_params=pltpu.CompilerParams(vmem_limit_bytes=6 * 1024 * 1024),
    )(r)


def body(grad_out, inputs, filt):
    turn = lax.axis_index("dp")
    wide = grad_out.shape[2]
    filter_turned = filt.T
    piece = lax.dynamic_slice(filter_turned, (0, 128 * (turn // 2)), (wide, 128))
    packed = jnp.concatenate([grad_out[0].T, inputs[0].T, piece], axis=1).reshape(128, 2, 640)
    arrived = lax.all_to_all(packed, ("context", "dp"), 0, 0, tiled=True)
    lanes = arrived.astype(F32).reshape(256, 5, 128).transpose(1, 0, 2).reshape(1280, 128)
    dx, dh = conv_call(lanes)
    dx = dx.reshape(2, 128, 2, 128).transpose(1, 2, 0, 3).reshape(128, 2, 256)
    dh = dh.reshape(2, 32, 2, 128).transpose(1, 2, 0, 3).reshape(32, 1, 2, 256)
    dh = jnp.broadcast_to(dh, (32, 4, 2, 256)).reshape(128, 2, 256)
    upper = lax.reduce_precision(dh, 8, 7)
    lower = (dh - upper).astype(BF16)
    outgoing = jnp.concatenate([dx.astype(BF16), upper.astype(BF16), lower], axis=2)
    returned = lax.all_to_all(outgoing, ("context", "dp"), 0, 0, tiled=True).reshape(256, 768)
    input_grad = returned[:, 0:256].T
    filter_grad = returned[:, 256:512].astype(F32) + returned[:, 512:768].astype(F32)
    return input_grad[None], filter_grad.T


def solution(mesh):
    return jax.shard_map(
        body,
        mesh=mesh,
        in_specs=(
            P("dp", "context", "tensor"),
            P("dp", "context", "tensor"),
            P("context", "tensor"),
        ),
        out_specs=(P("dp", "context", "tensor"), P("context", "tensor")),
        check_vma=False,
    )
```

```python
import functools
import jax
import jax.numpy as jnp
from jax import lax
from jax.experimental import pallas as pl
from jax.experimental.pallas import tpu as pltpu
from jax.sharding import PartitionSpec as P

F32 = jnp.float32
BF16 = jnp.bfloat16


def nt_dot(left, right):
    return lax.dot_general(left, right, (((1,), (1,)), ((), ())), preferred_element_type=F32)


def spread_row(ref, row, lane):
    return ref[pl.ds(2 * lane + row, 8, stride=0), :]


def lag_pieces(rows, out_ref):
    sub = lax.broadcasted_iota(jnp.int32, (8, 128), 0)
    lane = lax.broadcasted_iota(jnp.int32, (8, 128), 1)
    masks = [lane < sub + 8 * s for s in range(2)]
    before = [jnp.zeros((8, 128), F32) for _ in range(2)]
    for d in range(32):
        low, high = rows(d)
        pieces = []
        for s in range(2):
            low_turned = pltpu.roll(low, 8 * s, 1, stride=1, stride_axis=0)
            high_turned = pltpu.roll(high, 8 * s, 1, stride=1, stride_axis=0)
            pieces.append(
                jnp.concatenate(
                    [
                        jnp.where(masks[s], before[s], low_turned),
                        jnp.where(masks[s], low_turned, high_turned),
                    ],
                    axis=1,
                )
            )
            before[s] = high_turned
        out_ref[16 * d : 16 * d + 16, :] = jnp.concatenate(pieces, axis=0).astype(BF16)
        yield


def window_pieces(rows, out_ref, b):
    sub = lax.broadcasted_iota(jnp.int32, (8, 128), 0)
    lane = lax.broadcasted_iota(jnp.int32, (8, 128), 1)
    inside = lane < 16 + 16 * sub

    def turned(a):
        if a == 32:
            return [jnp.zeros((8, 128), F32)] * 2
        return [pltpu.roll(half, 16, 1, stride=16, stride_axis=0) for half in rows(a)]

    here = turned(0)
    first = jnp.where(inside, here[0], here[1])
    for a in range(32):
        after = turned(a + 1)
        second = jnp.where(inside, here[1], after[0])
        third = jnp.where(inside, after[0], after[1])
        block = jnp.concatenate(
            [
                jnp.concatenate([first, second], axis=1),
                jnp.concatenate([second, third], axis=1),
            ],
            axis=0,
        )
        out_ref[a, b] = block.astype(BF16)
        here, first = after, third
        yield


def product_pieces(left, lag_ref, total_ref, size, fresh):
    for q in range(2):
        part = nt_dot(left(16 * q), lag_ref[256 * q : 256 * q + 256, :])
        count = (32 - 16 * q) * size
        if fresh and q == 0:
            total_ref[0:count, :] = part[:, 0:128]
        else:
            total_ref[0:count, :] += part[:, 0:128]
        total_ref[0 : count - 8 * size, :] += part[8 * size :, 128:256]
        yield


def finish_pieces(total_ref, flat_ref, size, store):
    sub = lax.broadcasted_iota(jnp.int32, (8, 128), 0)
    lane = lax.broadcasted_iota(jnp.int32, (8, 128), 1)
    group = lane // 16
    keep = group == 7 - sub
    odd = [lax.rem(group // step, 2) == 1 for step in (1, 2, 4)]
    for rest in range(0, size, 8):

        def at(a):
            return total_ref[a * size + rest : a * size + rest + 8, :]

        ones, twos = {}, {}

        def one(a):
            if a not in ones:
                ones[a] = jnp.where(odd[0], at(a + 1), at(a))
            return ones[a]

        def two(a):
            if a not in twos:
                twos[a] = jnp.where(odd[1], one(a + 2), one(a))
            return twos[a]

        for a in range(32):
            row = a * size + rest
            flat_ref[row : row + 8, :] = jnp.where(odd[2], two(a + 4), two(a))
            if a % 8 == 7:
                yield
    keep_all = lax.broadcasted_iota(jnp.int32, (256, 128), 1) // 16 == 7 - lax.rem(
        lax.broadcasted_iota(jnp.int32, (256, 128), 0), 8
    )
    for turn in (64, 32, 16):
        for at in range(0, 32 * size, 256):
            mixed = flat_ref[at : at + 256, :]
            mixed = mixed + pltpu.roll(mixed, turn, 1)
            flat_ref[at : at + 256, :] = jnp.where(keep_all, mixed, 0.0) if turn == 16 else mixed
            yield
    for half in range(2):
        count = 2 * size
        store(
            half,
            sum(flat_ref[pl.ds(8 * half + i, count, stride=16), :] for i in range(8)),
        )
    yield


def interleave(*streams):
    done = [0] * len(streams)
    total = max(count for _, count in streams)
    for tick in range(1, total + 1):
        for at, (stream, count) in enumerate(streams):
            while done[at] * total < tick * count:
                next(stream)
                done[at] += 1
    for stream, _ in streams:
        for _ in stream:
            pass


def conv_kernel(r_ref, dx_ref, dh_ref, *scratch):
    window = scratch[0:2]
    lag_f = scratch[2:4]
    lag_x = scratch[4:8]
    total_dx = scratch[8:10]
    total_dh = scratch[10:12]
    flat_dx, flat_dh = scratch[12:14]

    def rows_of(part, shift):
        def rows(d):
            row = 8 * d + shift
            return (spread_row(r_ref, row, 128 * part), spread_row(r_ref, row, 128 * part + 128))

        return rows

    def filter_rows(c):
        def rows(d):
            return (spread_row(r_ref, 8 * d + c, 512), spread_row(r_ref, 8 * d + 4 + c, 512))

        return rows

    def signal_builds(c):
        builds = [(lag_pieces(filter_rows(c), lag_f[c]), 32)]
        for b in range(4):
            builds.append((window_pieces(rows_of(0, 2 * b + c), window[c], b), 32))
        return builds

    def lag_builds(c):
        return [(lag_pieces(rows_of(2, 2 * b + c), lag_x[b]), 32) for b in range(4)]

    def dx_products(c):
        def left(first):
            return window[c][first:].reshape((32 - first) * 64, 256)

        return (product_pieces(left, lag_f[c], total_dx[c], 64, True), 2)

    def dh_products(c):
        def chain():
            for b in range(4):

                def left(first):
                    return window[c][first:, b].reshape((32 - first) * 16, 256)

                yield from product_pieces(left, lag_x[b], total_dh[c], 16, b == 0)

        return (chain(), 8)

    def dx_finish(c):
        def store(half, rows):
            dx_ref[pl.ds(256 * half + c, 128, stride=2), :] = rows

        return (finish_pieces(total_dx[c], flat_dx, 64, store), 57)

    def dh_finish(c):
        def store(half, rows):
            dh_ref[pl.ds(64 * half + c, 32, stride=2), :] = rows

        return (finish_pieces(total_dh[c], flat_dh, 16, store), 15)

    for c in range(2):
        total_dx[c][2048:, :] = jnp.zeros((448, 128), F32)
        total_dh[c][512:, :] = jnp.zeros((112, 128), F32)
    interleave(*signal_builds(0))
    interleave(dx_products(0), *lag_builds(0))
    interleave(dh_products(0), *signal_builds(1), dx_finish(0))
    interleave(dx_products(1), *lag_builds(1), dh_finish(0))
    interleave(dh_products(1), dx_finish(1))
    interleave(dh_finish(1))


def conv_call(r):
    vmem = pl.BlockSpec(memory_space=pltpu.VMEM)
    return pl.pallas_call(
        conv_kernel,
        out_shape=(
            jax.ShapeDtypeStruct((512, 128), F32),
            jax.ShapeDtypeStruct((128, 128), F32),
        ),
        in_specs=[vmem],
        out_specs=(vmem, vmem),
        scratch_shapes=[pltpu.VMEM((32, 4, 16, 256), BF16)] * 2
        + [pltpu.VMEM((512, 256), BF16)] * 6
        + [pltpu.VMEM((2496, 128), F32)] * 2
        + [pltpu.VMEM((624, 128), F32)] * 2
        + [pltpu.VMEM((2048, 128), F32), pltpu.VMEM((512, 128), F32)],
        compiler_params=pltpu.CompilerParams(vmem_limit_bytes=24 * 1024 * 1024),
    )(r)


def body(grad_out, inputs, filt):
    turn = lax.axis_index("dp")
    wide = grad_out.shape[2]
    filter_turned = filt.T
    piece = lax.dynamic_slice(filter_turned, (0, 128 * (turn // 2)), (wide, 128))
    packed = jnp.concatenate([grad_out[0].T, inputs[0].T, piece], axis=1).reshape(128, 2, 640)
    arrived = lax.all_to_all(packed, ("context", "dp"), 0, 0, tiled=True)
    lanes = arrived.astype(F32).reshape(256, 5, 128).transpose(1, 0, 2).reshape(1280, 128)
    dx, dh = conv_call(lanes)
    dx = dx.reshape(2, 128, 2, 128).transpose(1, 2, 0, 3).reshape(128, 2, 256)
    dh = dh.reshape(2, 32, 2, 128).transpose(1, 2, 0, 3).reshape(32, 1, 2, 256)
    dh = jnp.broadcast_to(dh, (32, 4, 2, 256)).reshape(128, 2, 256)
    upper = lax.reduce_precision(dh, 8, 7)
    lower = (dh - upper).astype(BF16)
    outgoing = jnp.concatenate([dx.astype(BF16), upper.astype(BF16), lower], axis=2)
    returned = lax.all_to_all(outgoing, ("context", "dp"), 0, 0, tiled=True).reshape(256, 768)
    input_grad = returned[:, 0:256].T
    filter_grad = returned[:, 256:512].astype(F32) + returned[:, 512:768].astype(F32)
    return input_grad[None], filter_grad.T


def solution(mesh):
    return jax.shard_map(
        body,
        mesh=mesh,
        in_specs=(
            P("dp", "context", "tensor"),
            P("dp", "context", "tensor"),
            P("context", "tensor"),
        ),
        out_specs=(P("dp", "context", "tensor"), P("context", "tensor")),
        check_vma=False,
    )
```

```python
import functools
import jax
import jax.numpy as jnp
from jax import lax
from jax.experimental import pallas as pl
from jax.experimental.pallas import tpu as pltpu
from jax.sharding import PartitionSpec as P

F32 = jnp.float32
BF16 = jnp.bfloat16


def nt_dot(left, right):
    return lax.dot_general(left, right, (((1,), (1,)), ((), ())), preferred_element_type=F32)


def spread_row(ref, row, lane):
    return ref[pl.ds(2 * lane + row, 8, stride=0), :]


def lag_pieces(rows, out_ref):
    sub = lax.broadcasted_iota(jnp.int32, (8, 128), 0)
    lane = lax.broadcasted_iota(jnp.int32, (8, 128), 1)
    masks = [lane < sub + 8 * s for s in range(2)]
    before = [jnp.zeros((8, 128), F32) for _ in range(2)]
    for d in range(32):
        low, high = rows(d)
        pieces = []
        for s in range(2):
            low_turned = pltpu.roll(low, 8 * s, 1, stride=1, stride_axis=0)
            high_turned = pltpu.roll(high, 8 * s, 1, stride=1, stride_axis=0)
            pieces.append(
                jnp.concatenate(
                    [
                        jnp.where(masks[s], before[s], low_turned),
                        jnp.where(masks[s], low_turned, high_turned),
                    ],
                    axis=1,
                )
            )
            before[s] = high_turned
        out_ref[16 * d : 16 * d + 16, :] = jnp.concatenate(pieces, axis=0).astype(BF16)
        yield


def window_pieces(rows, out_ref, b):
    sub = lax.broadcasted_iota(jnp.int32, (8, 128), 0)
    lane = lax.broadcasted_iota(jnp.int32, (8, 128), 1)
    inside = lane < 16 + 16 * sub

    def turned(a):
        if a == 32:
            return [jnp.zeros((8, 128), F32)] * 2
        return [pltpu.roll(half, 16, 1, stride=16, stride_axis=0) for half in rows(a)]

    here = turned(0)
    first = jnp.where(inside, here[0], here[1])
    for a in range(32):
        after = turned(a + 1)
        second = jnp.where(inside, here[1], after[0])
        third = jnp.where(inside, after[0], after[1])
        block = jnp.concatenate(
            [
                jnp.concatenate([first, second], axis=1),
                jnp.concatenate([second, third], axis=1),
            ],
            axis=0,
        )
        out_ref[a, b] = block.astype(BF16)
        here, first = after, third
        yield


def product_pieces(left, lag_ref, total_ref, size, fresh):
    for q in range(2):
        part = nt_dot(left(16 * q), lag_ref[256 * q : 256 * q + 256, :])
        count = (32 - 16 * q) * size
        if fresh and q == 0:
            total_ref[0:count, :] = part[:, 0:128]
        else:
            total_ref[0:count, :] += part[:, 0:128]
        total_ref[0 : count - 8 * size, :] += part[8 * size :, 128:256]
        yield


def finish_pieces(total_ref, flat_ref, size, store):
    sub = lax.broadcasted_iota(jnp.int32, (8, 128), 0)
    lane = lax.broadcasted_iota(jnp.int32, (8, 128), 1)
    group = lane // 16
    keep = group == 7 - sub
    odd = [lax.rem(group // step, 2) == 1 for step in (1, 2, 4)]
    for rest in range(0, size, 8):

        def at(a):
            return total_ref[a * size + rest : a * size + rest + 8, :]

        ones, twos = {}, {}

        def one(a):
            if a not in ones:
                ones[a] = jnp.where(odd[0], at(a + 1), at(a))
            return ones[a]

        def two(a):
            if a not in twos:
                twos[a] = jnp.where(odd[1], one(a + 2), one(a))
            return twos[a]

        for a in range(32):
            row = a * size + rest
            flat_ref[row : row + 8, :] = jnp.where(odd[2], two(a + 4), two(a))
            if a % 8 == 7:
                yield
    keep_all = lax.broadcasted_iota(jnp.int32, (256, 128), 1) // 16 == 7 - lax.rem(
        lax.broadcasted_iota(jnp.int32, (256, 128), 0), 8
    )
    for turn in (64, 32, 16):
        for at in range(0, 32 * size, 256):
            mixed = flat_ref[at : at + 256, :]
            mixed = mixed + pltpu.roll(mixed, turn, 1)
            flat_ref[at : at + 256, :] = jnp.where(keep_all, mixed, 0.0) if turn == 16 else mixed
            yield
    for half in range(2):
        count = 2 * size
        store(
            half,
            sum(flat_ref[pl.ds(8 * half + i, count, stride=16), :] for i in range(8)),
        )
    yield


def interleave(*streams):
    done = [0] * len(streams)
    total = max(count for _, count in streams)
    for tick in range(1, total + 1):
        for at, (stream, count) in enumerate(streams):
            while done[at] * total < tick * count:
                next(stream)
                done[at] += 1
    for stream, _ in streams:
        for _ in stream:
            pass


def conv_kernel(r_ref, out_ref, *scratch):
    window = scratch[0:2]
    lag_f = scratch[2:4]
    lag_x = scratch[4:8]
    total_dx = scratch[8:10]
    total_dh = scratch[10:12]
    flat_dx, flat_dh = scratch[12:14]
    dx_ref, dh_ref = scratch[14:16]

    def rows_of(part, shift):
        def rows(d):
            row = 8 * d + shift
            return (spread_row(r_ref, row, 128 * part), spread_row(r_ref, row, 128 * part + 128))

        return rows

    def filter_rows(c):
        def rows(d):
            return (spread_row(r_ref, 8 * d + c, 512), spread_row(r_ref, 8 * d + 4 + c, 512))

        return rows

    def signal_builds(c):
        builds = [(lag_pieces(filter_rows(c), lag_f[c]), 32)]
        for b in range(4):
            builds.append((window_pieces(rows_of(0, 2 * b + c), window[c], b), 32))
        return builds

    def lag_builds(c):
        return [(lag_pieces(rows_of(2, 2 * b + c), lag_x[b]), 32) for b in range(4)]

    def dx_products(c):
        def left(first):
            return window[c][first:].reshape((32 - first) * 64, 256)

        return (product_pieces(left, lag_f[c], total_dx[c], 64, True), 2)

    def dh_products(c):
        def chain():
            for b in range(4):

                def left(first):
                    return window[c][first:, b].reshape((32 - first) * 16, 256)

                yield from product_pieces(left, lag_x[b], total_dh[c], 16, b == 0)

        return (chain(), 8)

    def dx_finish(c):
        def store(half, rows):
            dx_ref[pl.ds(256 * half + c, 128, stride=2), :] = rows

        return (finish_pieces(total_dx[c], flat_dx, 64, store), 57)

    def dh_finish(c):
        def store(half, rows):
            for b in range(4):
                dh_ref[pl.ds(256 * half + 2 * b + c, 32, stride=8), :] = rows

        return (finish_pieces(total_dh[c], flat_dh, 16, store), 15)

    for c in range(2):
        total_dx[c][2048:, :] = jnp.zeros((448, 128), F32)
        total_dh[c][512:, :] = jnp.zeros((112, 128), F32)
    interleave(*signal_builds(0))
    interleave(dx_products(0), *lag_builds(0))
    interleave(dh_products(0), *signal_builds(1), dx_finish(0))
    interleave(dx_products(1), *lag_builds(1), dh_finish(0))
    interleave(dh_products(1), dx_finish(1))
    interleave(dh_finish(1))
    for half in range(2):
        rows, lanes = slice(256 * half, 256 * half + 256), slice(128 * half, 128 * half + 128)
        out_ref[:, lanes] = dx_ref[rows, :].astype(BF16)
        total = dh_ref[rows, :]
        upper = total.astype(BF16)
        out_ref[:, 256 + 128 * half : 384 + 128 * half] = upper
        out_ref[:, 512 + 128 * half : 640 + 128 * half] = (total - upper.astype(F32)).astype(BF16)


def conv_call(r):
    vmem = pl.BlockSpec(memory_space=pltpu.VMEM)
    return pl.pallas_call(
        conv_kernel,
        out_shape=jax.ShapeDtypeStruct((256, 768), BF16),
        in_specs=[vmem],
        out_specs=vmem,
        scratch_shapes=[pltpu.VMEM((32, 4, 16, 256), BF16)] * 2
        + [pltpu.VMEM((512, 256), BF16)] * 6
        + [pltpu.VMEM((2496, 128), F32)] * 2
        + [pltpu.VMEM((624, 128), F32)] * 2
        + [pltpu.VMEM((2048, 128), F32), pltpu.VMEM((512, 128), F32)]
        + [pltpu.VMEM((512, 128), F32)] * 2,
        compiler_params=pltpu.CompilerParams(vmem_limit_bytes=24 * 1024 * 1024),
    )(r)


def unpack_kernel(r_ref, dx_hbm, dh_hbm, dx_ref, dh_ref, sems):
    dh_ref[...] = (r_ref[:, 256:512].astype(F32) + r_ref[:, 512:768].astype(F32)).T
    dh_copy = pltpu.make_async_copy(dh_ref, dh_hbm, sems.at[0])
    dh_copy.start()
    dx_ref[...] = r_ref[:, 0:256].T
    dx_copy = pltpu.make_async_copy(dx_ref, dx_hbm.at[0], sems.at[1])
    dx_copy.start()
    dh_copy.wait()
    dx_copy.wait()


def unpack_call(returned):
    hbm = pl.BlockSpec(memory_space=pl.ANY)
    return pl.pallas_call(
        unpack_kernel,
        out_shape=(
            jax.ShapeDtypeStruct((1, 256, 256), BF16),
            jax.ShapeDtypeStruct((256, 256), F32),
        ),
        in_specs=[pl.BlockSpec(memory_space=pltpu.VMEM)],
        out_specs=(hbm, hbm),
        scratch_shapes=[
            pltpu.VMEM((256, 256), BF16),
            pltpu.VMEM((256, 256), F32),
            pltpu.SemaphoreType.DMA((2,)),
        ],
        compiler_params=pltpu.CompilerParams(vmem_limit_bytes=4 * 1024 * 1024),
    )(returned)


def body(grad_out, inputs, filt):
    turn = lax.axis_index("dp")
    both = lax.optimization_barrier(jnp.concatenate([grad_out[0], inputs[0]], axis=0))
    piece = lax.dynamic_slice(filt, (128 * (turn // 2), 0), (128, 256))
    packed = jnp.concatenate([both, piece], axis=0).T.reshape(128, 2, 640)
    arrived = lax.all_to_all(packed, ("context", "dp"), 0, 0, tiled=True)
    lanes = arrived.astype(F32).reshape(256, 5, 128).transpose(1, 0, 2).reshape(1280, 128)
    outgoing = conv_call(lanes).reshape(128, 2, 768)
    returned = lax.all_to_all(outgoing, ("context", "dp"), 0, 0, tiled=True)
    return unpack_call(returned.reshape(256, 768))


def solution(mesh):
    return jax.shard_map(
        body,
        mesh=mesh,
        in_specs=(
            P("dp", "context", "tensor"),
            P("dp", "context", "tensor"),
            P("context", "tensor"),
        ),
        out_specs=(P("dp", "context", "tensor"), P("context", "tensor")),
        check_vma=False,
    )
```

```python
import itertools

import jax
import jax.numpy as jnp
from jax import lax
from jax.experimental import pallas as pl
from jax.experimental.pallas import tpu as pltpu
from jax.sharding import PartitionSpec as P

F32 = jnp.float32
BF16 = jnp.bfloat16


def nt_dot(left, right):
    return lax.dot_general(left, right, (((1,), (1,)), ((), ())), preferred_element_type=F32)


def spread_row(ref, row, lane):
    return ref[pl.ds(2 * lane + row, 8, stride=0), :]


def lag_pieces(rows, out_ref):
    sub = lax.broadcasted_iota(jnp.int32, (8, 128), 0)
    lane = lax.broadcasted_iota(jnp.int32, (8, 128), 1)
    masks = [lane < sub + 8 * s for s in range(2)]
    before = [jnp.zeros((8, 128), F32) for _ in range(2)]
    for d in range(32):
        low, high = rows(d)
        pieces = []
        for s in range(2):
            low_turned = pltpu.roll(low, 8 * s, 1, stride=1, stride_axis=0)
            high_turned = pltpu.roll(high, 8 * s, 1, stride=1, stride_axis=0)
            pieces.append(
                jnp.concatenate(
                    [
                        jnp.where(masks[s], before[s], low_turned),
                        jnp.where(masks[s], low_turned, high_turned),
                    ],
                    axis=1,
                )
            )
            before[s] = high_turned
        out_ref[16 * d : 16 * d + 16, :] = jnp.concatenate(pieces, axis=0).astype(BF16)
        yield


def window_pieces(rows, out_ref, b):
    sub = lax.broadcasted_iota(jnp.int32, (8, 128), 0)
    lane = lax.broadcasted_iota(jnp.int32, (8, 128), 1)
    inside = lane < 16 + 16 * sub

    def turned(a):
        if a == 32:
            return [jnp.zeros((8, 128), F32)] * 2
        return [pltpu.roll(half, 16, 1, stride=16, stride_axis=0) for half in rows(a)]

    here = turned(0)
    first = jnp.where(inside, here[0], here[1])
    for a in range(32):
        after = turned(a + 1)
        second = jnp.where(inside, here[1], after[0])
        third = jnp.where(inside, after[0], after[1])
        block = jnp.concatenate(
            [
                jnp.concatenate([first, second], axis=1),
                jnp.concatenate([second, third], axis=1),
            ],
            axis=0,
        )
        out_ref[a, b] = block.astype(BF16)
        here, first = after, third
        yield


def product_pieces(left, lag_ref, total_ref, size, fresh):
    for q in range(2):
        part = nt_dot(left(16 * q), lag_ref[256 * q : 256 * q + 256, :])
        count = (32 - 16 * q) * size
        if fresh and q == 0:
            total_ref[0:count, :] = part[:, 0:128]
        else:
            total_ref[0:count, :] += part[:, 0:128]
        total_ref[0 : count - 8 * size, :] += part[8 * size :, 128:256]
        yield


def finish_pieces(total_ref, flat_ref, size, store):
    group = lax.broadcasted_iota(jnp.int32, (8, 128), 1) // 16
    odd = [lax.rem(group // step, 2) == 1 for step in (1, 2, 4)]
    for rest in range(0, size, 8):

        def at(a):
            return total_ref[a * size + rest : a * size + rest + 8, :]

        ones, twos = {}, {}

        def one(a):
            if a not in ones:
                ones[a] = jnp.where(odd[0], at(a + 1), at(a))
            return ones[a]

        def two(a):
            if a not in twos:
                twos[a] = jnp.where(odd[1], one(a + 2), one(a))
            return twos[a]

        for a in range(32):
            row = a * size + rest
            flat_ref[row : row + 8, :] = jnp.where(odd[2], two(a + 4), two(a))
            if a % 8 == 7:
                yield
    count = min(2 * size, 32)
    wide_group = lax.broadcasted_iota(jnp.int32, (count, 128), 1) // 16
    wide_odd = [lax.rem(wide_group // step, 2) == 1 for step in (1, 2, 4)]
    for half in range(2):
        for first in range(0, 2 * size, count):
            base = 16 * first + 8 * half + 7
            terms = [flat_ref[pl.ds(base - (-k) % 8, count, stride=16), :] for k in range(8)]
            for mask, step in zip(wide_odd, (1, 2, 4)):
                terms = [jnp.where(mask, terms[(k - step) % 8], terms[k]) for k in range(8)]
            for turn in (16, 32, 64):
                terms = [
                    terms[k] + pltpu.roll(terms[k + 1], 128 - turn, 1) for k in range(0, len(terms), 2)
                ]
            store(half, first, terms[0])
            yield


def interleave(*streams):
    done = [0] * len(streams)
    total = max(count for _, count in streams)
    for tick in range(1, total + 1):
        for at, (stream, count) in enumerate(streams):
            while done[at] * total < tick * count:
                next(stream)
                done[at] += 1
    for stream, _ in streams:
        for _ in stream:
            pass


def conv_kernel(r_ref, out_ref, *scratch):
    window = scratch[0:2]
    lag_f = scratch[2:4]
    lag_x = scratch[4:8]
    total_dx = scratch[8:10]
    total_dh = scratch[10:12]
    flat_dx, flat_dh = scratch[12:14]
    dx_ref, dh_ref = scratch[14:16]

    def rows_of(part, shift):
        def rows(d):
            row = 8 * d + shift
            return (spread_row(r_ref, row, 128 * part), spread_row(r_ref, row, 128 * part + 128))

        return rows

    def filter_rows(c):
        def rows(d):
            return (spread_row(r_ref, 8 * d + c, 512), spread_row(r_ref, 8 * d + 4 + c, 512))

        return rows

    def window_build(c, b):
        return (window_pieces(rows_of(0, 2 * b + c), window[c], b), 32)

    def lag_build(c, b):
        return (lag_pieces(rows_of(2, 2 * b + c), lag_x[b]), 32)

    def filter_build(c):
        return (lag_pieces(filter_rows(c), lag_f[c]), 32)

    def dx_products(c):
        def left(first):
            return window[c][first:].reshape((32 - first) * 64, 256)

        return (product_pieces(left, lag_f[c], total_dx[c], 64, True), 2)

    def dh_products(c, b):
        def left(first):
            return window[c][first:, b].reshape((32 - first) * 16, 256)

        return (product_pieces(left, lag_x[b], total_dh[c], 16, b == 0), 2)

    def dx_finish(c):
        def store(half, first, rows):
            dx_ref[pl.ds(256 * half + 2 * first + c, rows.shape[0], stride=2), :] = rows

        return (finish_pieces(total_dx[c], flat_dx, 64, store), 40)

    def dh_finish(c):
        def store(half, first, rows):
            for b in range(4):
                row = 256 * half + 8 * first + 2 * b + c
                dh_ref[pl.ds(row, rows.shape[0], stride=8), :] = rows

        return (finish_pieces(total_dh[c], flat_dh, 16, store), 10)

    for c in range(2):
        total_dx[c][2048:, :] = jnp.zeros((448, 128), F32)
        total_dh[c][512:, :] = jnp.zeros((112, 128), F32)
    interleave(window_build(0, 0), lag_build(0, 0))
    for b in range(3):
        interleave(dh_products(0, b), window_build(0, b + 1), lag_build(0, b + 1))
    interleave(dh_products(0, 3), filter_build(0), window_build(1, 0))
    later = [window_build(1, b) for b in range(1, 4)]
    interleave(dx_products(0), filter_build(1), *later, dh_finish(0))
    interleave(dx_products(1), *[lag_build(1, b) for b in range(4)], dx_finish(0))
    last = [dh_products(1, b) for b in range(4)]
    interleave((itertools.chain(*[pieces for pieces, _ in last]), 8), dx_finish(1))
    interleave(dh_finish(1))
    for half in range(2):
        rows, lanes = slice(256 * half, 256 * half + 256), slice(128 * half, 128 * half + 128)
        out_ref[:, lanes] = dx_ref[rows, :].astype(BF16)
        total = dh_ref[rows, :]
        upper = total.astype(BF16)
        out_ref[:, 256 + 128 * half : 384 + 128 * half] = upper
        out_ref[:, 512 + 128 * half : 640 + 128 * half] = (total - upper.astype(F32)).astype(BF16)


def conv_call(r):
    vmem = pl.BlockSpec(memory_space=pltpu.VMEM)
    return pl.pallas_call(
        conv_kernel,
        out_shape=jax.ShapeDtypeStruct((256, 768), BF16),
        in_specs=[vmem],
        out_specs=vmem,
        scratch_shapes=[pltpu.VMEM((32, 4, 16, 256), BF16)] * 2
        + [pltpu.VMEM((512, 256), BF16)] * 6
        + [pltpu.VMEM((2496, 128), F32)] * 2
        + [pltpu.VMEM((624, 128), F32)] * 2
        + [pltpu.VMEM((2048, 128), F32), pltpu.VMEM((512, 128), F32)]
        + [pltpu.VMEM((512, 128), F32)] * 2,
        compiler_params=pltpu.CompilerParams(vmem_limit_bytes=24 * 1024 * 1024),
    )(r)


def unpack_kernel(r_ref, dx_hbm, dh_hbm, dx_ref, dh_ref, sems):
    dh_ref[...] = (r_ref[:, 256:512].astype(F32) + r_ref[:, 512:768].astype(F32)).T
    dh_copy = pltpu.make_async_copy(dh_ref, dh_hbm, sems.at[0])
    dh_copy.start()
    dx_ref[...] = r_ref[:, 0:256].T
    dx_copy = pltpu.make_async_copy(dx_ref, dx_hbm.at[0], sems.at[1])
    dx_copy.start()
    dh_copy.wait()
    dx_copy.wait()


def unpack_call(returned):
    hbm = pl.BlockSpec(memory_space=pl.ANY)
    return pl.pallas_call(
        unpack_kernel,
        out_shape=(
            jax.ShapeDtypeStruct((1, 256, 256), BF16),
            jax.ShapeDtypeStruct((256, 256), F32),
        ),
        in_specs=[pl.BlockSpec(memory_space=pltpu.VMEM)],
        out_specs=(hbm, hbm),
        scratch_shapes=[
            pltpu.VMEM((256, 256), BF16),
            pltpu.VMEM((256, 256), F32),
            pltpu.SemaphoreType.DMA((2,)),
        ],
        compiler_params=pltpu.CompilerParams(vmem_limit_bytes=4 * 1024 * 1024),
    )(returned)


def body(grad_out, inputs, filt):
    turn = lax.axis_index("dp")
    both = lax.optimization_barrier(jnp.concatenate([grad_out[0], inputs[0]], axis=0))
    piece = lax.dynamic_slice(filt, (128 * (turn // 2), 0), (128, 256))
    packed = jnp.concatenate([both, piece], axis=0).T.reshape(128, 2, 640)
    arrived = lax.all_to_all(packed, ("context", "dp"), 0, 0, tiled=True)
    lanes = arrived.astype(F32).reshape(256, 5, 128).transpose(1, 0, 2).reshape(1280, 128)
    outgoing = conv_call(lanes).reshape(128, 2, 768)
    returned = lax.all_to_all(outgoing, ("context", "dp"), 0, 0, tiled=True)
    return unpack_call(returned.reshape(256, 768))


def solution(mesh):
    return jax.shard_map(
        body,
        mesh=mesh,
        in_specs=(
            P("dp", "context", "tensor"),
            P("dp", "context", "tensor"),
            P("context", "tensor"),
        ),
        out_specs=(P("dp", "context", "tensor"), P("context", "tensor")),
        check_vma=False,
    )
```

```python
import itertools

import jax
import jax.numpy as jnp
from jax import lax
from jax.experimental import pallas as pl
from jax.experimental.pallas import tpu as pltpu
from jax.sharding import PartitionSpec as P

F32 = jnp.float32
BF16 = jnp.bfloat16


def nt_dot(left, right):
    return lax.dot_general(left, right, (((1,), (1,)), ((), ())), preferred_element_type=F32)


def spread_row(ref, row, lane):
    return jnp.broadcast_to(ref[row, lane // 128 : lane // 128 + 1, :], (8, 128))


def lag_pieces(rows, out_ref):
    sub = lax.broadcasted_iota(jnp.int32, (8, 128), 0)
    lane = lax.broadcasted_iota(jnp.int32, (8, 128), 1)
    masks = [lane < sub + 8 * s for s in range(2)]
    before = [jnp.zeros((8, 128), F32) for _ in range(2)]
    for d in range(32):
        low, high = rows(d)
        pieces = []
        for s in range(2):
            low_turned = pltpu.roll(low, 8 * s, 1, stride=1, stride_axis=0)
            high_turned = pltpu.roll(high, 8 * s, 1, stride=1, stride_axis=0)
            pieces.append(
                jnp.concatenate(
                    [
                        jnp.where(masks[s], before[s], low_turned),
                        jnp.where(masks[s], low_turned, high_turned),
                    ],
                    axis=1,
                )
            )
            before[s] = high_turned
        out_ref[16 * d : 16 * d + 16, :] = jnp.concatenate(pieces, axis=0).astype(BF16)
        yield


def window_pieces(rows, out_ref, b):
    sub = lax.broadcasted_iota(jnp.int32, (8, 128), 0)
    lane = lax.broadcasted_iota(jnp.int32, (8, 128), 1)
    inside = lane < 16 + 16 * sub

    def turned(a):
        if a == 32:
            return [jnp.zeros((8, 128), F32)] * 2
        return [pltpu.roll(half, 16, 1, stride=16, stride_axis=0) for half in rows(a)]

    here = turned(0)
    first = jnp.where(inside, here[0], here[1])
    for a in range(32):
        after = turned(a + 1)
        second = jnp.where(inside, here[1], after[0])
        third = jnp.where(inside, after[0], after[1])
        block = jnp.concatenate(
            [
                jnp.concatenate([first, second], axis=1),
                jnp.concatenate([second, third], axis=1),
            ],
            axis=0,
        )
        out_ref[a, b] = block.astype(BF16)
        here, first = after, third
        yield


def product_pieces(left, lag_ref, total_ref, size, fresh):
    for q in range(2):
        part = nt_dot(left(16 * q), lag_ref[256 * q : 256 * q + 256, :])
        count = (32 - 16 * q) * size
        if fresh and q == 0:
            total_ref[0:count, :] = part[:, 0:128]
        else:
            total_ref[0:count, :] += part[:, 0:128]
        total_ref[0 : count - 8 * size, :] += part[8 * size :, 128:256]
        yield


def finish_pieces(total_ref, flat_ref, size, store):
    group = lax.broadcasted_iota(jnp.int32, (8, 128), 1) // 16
    odd = [lax.rem(group // step, 2) == 1 for step in (1, 2, 4)]
    for rest in range(0, size, 8):

        def at(a):
            return total_ref[a * size + rest : a * size + rest + 8, :]

        ones, twos = {}, {}

        def one(a):
            if a not in ones:
                ones[a] = jnp.where(odd[0], at(a + 1), at(a))
            return ones[a]

        def two(a):
            if a not in twos:
                twos[a] = jnp.where(odd[1], one(a + 2), one(a))
            return twos[a]

        for a in range(32):
            row = a * size + rest
            flat_ref[row : row + 8, :] = jnp.where(odd[2], two(a + 4), two(a))
            if a % 8 == 7:
                yield
    count, step_rows = 32, size
    wide_group = lax.broadcasted_iota(jnp.int32, (count, 128), 1) // 16
    wide_odd = [lax.rem(wide_group // step, 2) == 1 for step in (1, 2, 4)]
    for half in range(2):
        for first in range(size // 16):
            base = 16 * first + 8 * half + 7
            terms = [flat_ref[pl.ds(base - (-k) % 8, count, stride=step_rows), :] for k in range(8)]
            for mask, step in zip(wide_odd, (1, 2, 4)):
                terms = [jnp.where(mask, terms[(k - step) % 8], terms[k]) for k in range(8)]
            for turn in (16, 32, 64):
                terms = [
                    terms[k] + pltpu.roll(terms[k + 1], 128 - turn, 1) for k in range(0, len(terms), 2)
                ]
            store(half, first, terms[0])
            yield


def interleave(*streams):
    done = [0] * len(streams)
    total = max(count for _, count in streams)
    for tick in range(1, total + 1):
        for at, (stream, count) in enumerate(streams):
            while done[at] * total < tick * count:
                next(stream)
                done[at] += 1
    for stream, _ in streams:
        for _ in stream:
            pass


def conv_kernel(r_ref, out_ref, *scratch):
    window = scratch[0:2]
    lag_f = scratch[2:4]
    lag_x = scratch[4:8]
    total_dx = scratch[8:10]
    total_dh = scratch[10:12]
    flat_dx, flat_dh = scratch[12:14]
    dx_ref, dh_ref = scratch[14:16]

    def rows_of(part, shift):
        def rows(d):
            row = 2 * d + shift
            return (spread_row(r_ref, row, 128 * part), spread_row(r_ref, row, 128 * part + 128))

        return rows

    def filter_rows(c):
        def rows(d):
            return (spread_row(r_ref, 2 * d + c, 512), spread_row(r_ref, 2 * d + 128 + c, 512))

        return rows

    def window_build(c, b):
        return (window_pieces(rows_of(0, 64 * b + c), window[c], b), 32)

    def lag_build(c, b):
        return (lag_pieces(rows_of(2, 64 * b + c), lag_x[b]), 32)

    def filter_build(c):
        return (lag_pieces(filter_rows(c), lag_f[c]), 32)

    def dx_products(c):
        def left(first):
            return window[c][first:].reshape((32 - first) * 64, 256)

        return (product_pieces(left, lag_f[c], total_dx[c], 64, True), 2)

    def dh_products(c, b):
        def left(first):
            return window[c][first:, b].reshape((32 - first) * 16, 256)

        return (product_pieces(left, lag_x[b], total_dh[c], 16, b == 0), 2)

    def dx_finish(c):
        def store(half, first, rows):
            dx_ref[pl.ds(256 * half + 64 * first + c, 32, stride=2), :] = rows

        return (finish_pieces(total_dx[c], flat_dx, 64, store), 40)

    def dh_finish(c):
        def store(half, first, rows):
            for b in range(4):
                dh_ref[pl.ds(256 * half + 64 * b + c, 32, stride=2), :] = rows

        return (finish_pieces(total_dh[c], flat_dh, 16, store), 10)

    for c in range(2):
        total_dx[c][2048:, :] = jnp.zeros((448, 128), F32)
        total_dh[c][512:, :] = jnp.zeros((112, 128), F32)
    interleave(window_build(0, 0), lag_build(0, 0))
    for b in range(3):
        interleave(dh_products(0, b), window_build(0, b + 1), lag_build(0, b + 1))
    interleave(dh_products(0, 3), filter_build(0), window_build(1, 0))
    later = [window_build(1, b) for b in range(1, 4)]
    interleave(dx_products(0), filter_build(1), *later, dh_finish(0))
    interleave(dx_products(1), *[lag_build(1, b) for b in range(4)], dx_finish(0))
    last = [dh_products(1, b) for b in range(4)]
    interleave((itertools.chain(*[pieces for pieces, _ in last]), 8), dx_finish(1))
    interleave(dh_finish(1))
    for half in range(2):
        rows, lanes = slice(256 * half, 256 * half + 256), slice(128 * half, 128 * half + 128)
        out_ref[:, lanes] = dx_ref[rows, :].astype(BF16)
        total = dh_ref[rows, :]
        upper = total.astype(BF16)
        out_ref[:, 256 + 128 * half : 384 + 128 * half] = upper
        out_ref[:, 512 + 128 * half : 640 + 128 * half] = (total - upper.astype(F32)).astype(BF16)


def conv_call(r):
    vmem = pl.BlockSpec(memory_space=pltpu.VMEM)
    return pl.pallas_call(
        conv_kernel,
        out_shape=jax.ShapeDtypeStruct((256, 768), BF16),
        in_specs=[vmem],
        out_specs=vmem,
        scratch_shapes=[pltpu.VMEM((32, 4, 16, 256), BF16)] * 2
        + [pltpu.VMEM((512, 256), BF16)] * 6
        + [pltpu.VMEM((2496, 128), F32)] * 2
        + [pltpu.VMEM((624, 128), F32)] * 2
        + [pltpu.VMEM((2048, 128), F32), pltpu.VMEM((512, 128), F32)]
        + [pltpu.VMEM((512, 128), F32)] * 2,
        compiler_params=pltpu.CompilerParams(vmem_limit_bytes=24 * 1024 * 1024),
    )(r)


def unpack_kernel(r_ref, dx_hbm, dh_hbm, dx_ref, dh_ref, sems):
    dh_ref[...] = (r_ref[:, 256:512].astype(F32) + r_ref[:, 512:768].astype(F32)).T
    dh_copy = pltpu.make_async_copy(dh_ref, dh_hbm, sems.at[0])
    dh_copy.start()
    dx_ref[...] = r_ref[:, 0:256].T
    dx_copy = pltpu.make_async_copy(dx_ref, dx_hbm.at[0], sems.at[1])
    dx_copy.start()
    dh_copy.wait()
    dx_copy.wait()


def unpack_call(returned):
    hbm = pl.BlockSpec(memory_space=pl.ANY)
    return pl.pallas_call(
        unpack_kernel,
        out_shape=(
            jax.ShapeDtypeStruct((1, 256, 256), BF16),
            jax.ShapeDtypeStruct((256, 256), F32),
        ),
        in_specs=[pl.BlockSpec(memory_space=pltpu.VMEM)],
        out_specs=(hbm, hbm),
        scratch_shapes=[
            pltpu.VMEM((256, 256), BF16),
            pltpu.VMEM((256, 256), F32),
            pltpu.SemaphoreType.DMA((2,)),
        ],
        compiler_params=pltpu.CompilerParams(vmem_limit_bytes=4 * 1024 * 1024),
    )(returned)


def body(grad_out, inputs, filt):
    turn = lax.axis_index("dp")
    both = lax.optimization_barrier(jnp.concatenate([grad_out[0], inputs[0]], axis=0))
    piece = lax.dynamic_slice(filt, (128 * (turn // 2), 0), (128, 256))
    packed = jnp.concatenate([both, piece], axis=0).T.reshape(128, 2, 640)
    arrived = lax.all_to_all(packed, ("dp", "context"), 0, 0, tiled=True)
    lanes = arrived.astype(F32).reshape(256, 5, 128)
    outgoing = conv_call(lanes).reshape(128, 2, 768)
    returned = lax.all_to_all(outgoing, ("dp", "context"), 0, 0, tiled=True)
    return unpack_call(returned.reshape(256, 768))


def solution(mesh):
    return jax.shard_map(
        body,
        mesh=mesh,
        in_specs=(
            P("dp", "context", "tensor"),
            P("dp", "context", "tensor"),
            P("context", "tensor"),
        ),
        out_specs=(P("dp", "context", "tensor"), P("context", "tensor")),
        check_vma=False,
    )
```
